32 devices in a mesh: req: 4 (over y, x), head: 8 (over z, core).
Axes of the slice: x: 2, y: 2, z: 4, core: 2. Of those that a mesh axis runs over, the one named last changes fastest.
Arguments:
- hidden: bfloat16 [4, 256, 5120], P('req', 'head'), may hold values from -6 to 6
- cached_len: int32 [4], P('req'), may hold values from 2 to 4096, as said below
- attn_gain: float32 [5120], replicated, may hold values from 0.5 to 1.5
- query_key_value_weight: bfloat16 [5120, 6144], P(None, 'head'), may hold values from -0.078125 to 0.078125
- b_qkv: bfloat16 [6144], P('head'), may hold values from -1.5 to 1.5
- key_cache: bfloat16 [4, 4096, 1024], P('req', 'head'), may hold values from -4000 to 4000
- value_cache: bfloat16 [4, 4096, 1024], P('req', 'head'), may hold values from -6 to 6
- w_out: bfloat16 [4096, 5120], P('head'), may hold values from -0.09375 to 0.09375
- ffn_gain: float32 [5120], replicated, may hold values from 0.5 to 1.5
- w_gate: bfloat16 [5120, 13824], P(None, 'head'), may hold values from -0.078125 to 0.078125
- w_up: bfloat16 [5120, 13824], P(None, 'head'), may hold values from -0.078125 to 0.078125
- w_down: bfloat16 [13824, 5120], P('head'), may hold values from -0.0546875 to 0.0546875
Outputs:
- layer_out: bfloat16 [4, 256, 5120], P('req', 'head')
- new_keys: bfloat16 [4, 256, 1024], P('req', 'head')
- new_values: bfloat16 [4, 256, 1024], P('req', 'head')
The draws below stay inside these ranges and needn't reach their ends.
Inputs may be any that keep to these rules, and one draw needn't show every extreme that they name: `cached_len`: about half of the requests have nearly full caches, within 512 of 4096, one of them exactly 4096; the others hold fewer than 512 positions; which requests are which is drawn.
All inputs are finite; a program needn't handle non-finite values.
Results may differ from the reference program's by a relative error of at most 0.015.
Values may be sent and summed in bfloat16 or wider, within the bound.
A program may use at most 256 MiB of HBM per device.

```python
import math
import jax
import jax.numpy as jnp
from jax import lax

MODEL_WIDTH = 5120
QUERY_HEADS = 32
KEY_VALUE_HEADS = 8
HEAD_WIDTH = 128
FF = 13824
FRESH_TOKENS = 256
CACHE_DEV = 512
CACHE_SLOTS = 4096
REQUEST_COUNT = 4


def bias_lookup(key):
    random_noise = 0.5 * jax.random.normal(jax.random.fold_in(key, 7), ((QUERY_HEADS + 2 * KEY_VALUE_HEADS) * HEAD_WIDTH,), jnp.float32)
    return jnp.clip(random_noise, -1.5, 1.5)


def draw_b_qkv(key, part):
    return bias_lookup(key).astype(jnp.bfloat16)


def draw_cached_len(key, part):
    ranking = jax.random.permutation(jax.random.fold_in(key, 3), REQUEST_COUNT)
    longer = CACHE_SLOTS - jax.random.randint(jax.random.fold_in(key, 4), (REQUEST_COUNT,), 0, CACHE_DEV)
    longer = jnp.where(ranking == 0, CACHE_SLOTS, longer)
    shorter = jax.random.randint(jax.random.fold_in(key, 5), (REQUEST_COUNT,), 2, CACHE_DEV)
    return jnp.where(ranking < max(REQUEST_COUNT // 2, 1), longer, shorter).astype(jnp.int32)


def draw_key_cache(key, part):
    array_shape = (REQUEST_COUNT, CACHE_SLOTS, KEY_VALUE_HEADS * HEAD_WIDTH)
    start_vals = jnp.clip(jax.random.normal(jax.random.fold_in(key, 11), array_shape, jnp.float32), -6.0, 6.0)
    return start_vals.astype(jnp.bfloat16)


def levels(rng, dims, cuts, low, largest):
    loudness = 1.0
    for dim, blocks in cuts:
        draws = jax.random.uniform(jax.random.fold_in(jax.random.fold_in(rng, 6), dim), (blocks,), jnp.float32, low / len(cuts), largest / len(cuts))
        loudness = loudness * jnp.repeat(jnp.exp(draws), dims[dim] // blocks).reshape((-1,) + (1,) * (len(dims) - 1 - dim))
    return loudness


def noise(key, extent, scale, limit, shards=(), kind=jnp.bfloat16):
    array = jax.random.normal(key, extent, jnp.float32) * scale
    if len(shards) > 0:
        array = levels(key, extent, shards, -0.22, 0.18) * array
    return jnp.clip(array, min=-limit, max=limit).astype(kind)


def setup_inputs(seed: int = 0) -> dict:
    splits = jax.random.split(jax.random.key(seed), 13)
    return {
        "hidden": noise(splits[0], (REQUEST_COUNT, FRESH_TOKENS, MODEL_WIDTH), 1.0, 6.0, ((0, 4), (1, 8))),
        "cached_len": draw_cached_len(jax.random.fold_in(splits[12], 71), 0),
        "attn_gain": jnp.clip(1.0 + 0.1 * jax.random.normal(splits[2], (MODEL_WIDTH,), jnp.float32), 0.5, 1.5),
        "query_key_value_weight": noise(splits[3], (MODEL_WIDTH, (QUERY_HEADS + 2 * KEY_VALUE_HEADS) * HEAD_WIDTH), MODEL_WIDTH ** -0.5, 0.078125, ((1, 8),)),
        "b_qkv": draw_b_qkv(jax.random.fold_in(splits[12], 71), 0),
        "key_cache": draw_key_cache(jax.random.fold_in(splits[12], 71), 0),
        "value_cache": noise(splits[6], (REQUEST_COUNT, CACHE_SLOTS, KEY_VALUE_HEADS * HEAD_WIDTH), 1.0, 6.0, ((0, 4), (1, 8))),
        "w_out": noise(splits[7], (QUERY_HEADS * HEAD_WIDTH, MODEL_WIDTH), (QUERY_HEADS * HEAD_WIDTH) ** -0.5, 0.09375, ((0, 8),)),
        "ffn_gain": jnp.clip(1.0 + 0.1 * jax.random.normal(splits[8], (MODEL_WIDTH,), jnp.float32), 0.5, 1.5),
        "w_gate": noise(splits[9], (MODEL_WIDTH, FF), MODEL_WIDTH ** -0.5, 0.078125, ((1, 8),)),
        "w_up": noise(splits[10], (MODEL_WIDTH, FF), MODEL_WIDTH ** -0.5, 0.078125, ((1, 8),)),
        "w_down": noise(splits[11], (FF, MODEL_WIDTH), FF ** -0.5, 0.0546875, ((0, 8),)),
    }


rope_base = 1000000.0

def rms_norm(values, gain):
    data = values.astype(jnp.float32)
    spread = lax.optimization_barrier(jnp.mean(data * data, axis=-1, keepdims=True))
    return (data * lax.rsqrt(spread + 1e-06) * gain.astype(jnp.float32)).astype(jnp.bfloat16)

def rope_apply(values, positions):
    half_dim = HEAD_WIDTH // 2
    inverse = rope_base ** (-(jnp.arange(half_dim, dtype=jnp.float32) * 2.0 / HEAD_WIDTH))
    angles = positions.astype(jnp.float32)[:, None] * inverse[None, :]
    cosine = jnp.concatenate([jnp.cos(angles), jnp.cos(angles)], axis=-1)[:, None, :]
    sine = jnp.concatenate([jnp.sin(angles), jnp.sin(angles)], axis=-1)[:, None, :]
    data = values.astype(jnp.float32)
    rotated = jnp.concatenate([-data[..., half_dim:], data[..., :half_dim]], axis=-1)
    return (data * cosine + rotated * sine).astype(jnp.bfloat16)

def reference(hidden, cached_len, attn_gain, query_key_value_weight, b_qkv, key_cache, value_cache, w_out, ffn_gain, w_gate, w_up, w_down):
    head_group = QUERY_HEADS // KEY_VALUE_HEADS
    scale = 1.0 / math.sqrt(HEAD_WIDTH)
    outputs = []
    key_pieces = []
    value_pieces = []
    for request_index in range(REQUEST_COUNT):
        inputs = hidden[request_index]
        normed = rms_norm(inputs, attn_gain)
        query_key_value = (jnp.dot(normed, query_key_value_weight, preferred_element_type=jnp.float32) + b_qkv.astype(jnp.float32)).astype(jnp.bfloat16)
        query_rows = query_key_value[:, :QUERY_HEADS * HEAD_WIDTH].reshape(FRESH_TOKENS, QUERY_HEADS, HEAD_WIDTH)
        fresh_keys = query_key_value[:, QUERY_HEADS * HEAD_WIDTH:(QUERY_HEADS + KEY_VALUE_HEADS) * HEAD_WIDTH].reshape(FRESH_TOKENS, KEY_VALUE_HEADS, HEAD_WIDTH)
        fresh_values = query_key_value[:, (QUERY_HEADS + KEY_VALUE_HEADS) * HEAD_WIDTH:].reshape(FRESH_TOKENS, KEY_VALUE_HEADS, HEAD_WIDTH)
        positions = cached_len[request_index] + jnp.arange(FRESH_TOKENS, dtype=jnp.int32)
        query_rows = rope_apply(query_rows, positions)
        fresh_keys = rope_apply(fresh_keys, positions)
        key_pieces.append(fresh_keys.reshape(FRESH_TOKENS, KEY_VALUE_HEADS * HEAD_WIDTH))
        value_pieces.append(fresh_values.reshape(FRESH_TOKENS, KEY_VALUE_HEADS * HEAD_WIDTH))
        cache_ok = jnp.arange(CACHE_SLOTS, dtype=jnp.int32) < cached_len[request_index]
        token_ids = jnp.arange(FRESH_TOKENS, dtype=jnp.int32)
        new_ok = token_ids[None, :] <= token_ids[:, None]
        allowed = jnp.concatenate([jnp.broadcast_to(cache_ok[None, :], (FRESH_TOKENS, CACHE_SLOTS)), new_ok], axis=1)
        query_head_rows = query_rows.reshape(FRESH_TOKENS, KEY_VALUE_HEADS, head_group, HEAD_WIDTH).transpose(1, 0, 2, 3)
        stored_keys = key_cache[request_index].reshape(CACHE_SLOTS, KEY_VALUE_HEADS, HEAD_WIDTH).transpose(1, 0, 2)
        stored_values = value_cache[request_index].reshape(CACHE_SLOTS, KEY_VALUE_HEADS, HEAD_WIDTH).transpose(1, 0, 2)

        def one_head(items):
            query_h, ckeys, cvalues, nkeys, nvalues = items
            joined_keys = jnp.concatenate([ckeys, nkeys], axis=0).astype(jnp.float32)
            joined_values = jnp.concatenate([cvalues, nvalues], axis=0).astype(jnp.float32)
            scores = jnp.einsum('tjd,sd->jts', query_h.astype(jnp.float32), joined_keys) * scale
            scores = jnp.where(allowed[None], scores, -1e+30)
            top = lax.optimization_barrier(jnp.max(scores, axis=-1, keepdims=True))
            expo = jnp.where(allowed[None], jnp.exp(scores - top), 0.0)
            total = lax.optimization_barrier(jnp.sum(expo, axis=-1))
            weights = expo.astype(jnp.bfloat16).astype(jnp.float32)
            mixed = jnp.einsum('jts,sd->tjd', weights, joined_values)
            return (mixed / jnp.transpose(total)[:, :, None]).astype(jnp.bfloat16)
        attended = lax.map(one_head, (query_head_rows, stored_keys, stored_values, fresh_keys.transpose(1, 0, 2), fresh_values.transpose(1, 0, 2)))
        attn = attended.transpose(1, 0, 2, 3).reshape(FRESH_TOKENS, QUERY_HEADS * HEAD_WIDTH)
        projected = jnp.dot(attn, w_out, preferred_element_type=jnp.float32)
        middle = (inputs.astype(jnp.float32) + projected).astype(jnp.bfloat16)
        normed_two = rms_norm(middle, ffn_gain)
        gate = jnp.dot(normed_two, w_gate, preferred_element_type=jnp.float32)
        upward = jnp.dot(normed_two, w_up, preferred_element_type=jnp.float32)
        active = (jax.nn.silu(gate) * upward).astype(jnp.bfloat16)
        result = middle.astype(jnp.float32) + jnp.dot(active, w_down, preferred_element_type=jnp.float32)
        outputs.append(result.astype(jnp.bfloat16))
    return (jnp.stack(outputs), jnp.stack(key_pieces), jnp.stack(value_pieces))
```

```python
import functools
import math

import jax
import jax.numpy as jnp
from jax import lax
from jax.experimental import pallas as pl
from jax.experimental.pallas import tpu as pltpu
from jax.sharding import PartitionSpec as P

QUERY_HEADS = 32
KEY_VALUE_HEADS = 8
HEAD_WIDTH = 128
GROUP = QUERY_HEADS // KEY_VALUE_HEADS
SCALE = 1.0 / math.sqrt(HEAD_WIDTH)
TAIL = 16

rope_base = 1000000.0
MESH = pl.DeviceIdType.MESH


def rms_norm(values, gain):
    data = values.astype(jnp.float32)
    spread = jnp.mean(data * data, axis=-1, keepdims=True)
    return (data * lax.rsqrt(spread + 1e-06) * gain).astype(jnp.bfloat16)


def rope_tables(positions):
    half_dim = HEAD_WIDTH // 2
    inverse = rope_base ** (-(jnp.arange(half_dim, dtype=jnp.float32) * 2.0 / HEAD_WIDTH))
    angles = positions.astype(jnp.float32)[:, None] * inverse[None, :]
    cosine = jnp.cos(angles)
    sine = jnp.sin(angles)
    return (
        jnp.concatenate([cosine, cosine], axis=-1),
        jnp.concatenate([-sine, sine], axis=-1),
    )


def chain_barrier(chips, me, chip, partner):
    barrier = pltpu.get_barrier_semaphore()
    pl.semaphore_signal(barrier, inc=1, device_id={"head": partner}, device_id_type=MESH)

    @pl.when(chip > 0)
    def _():
        pl.semaphore_signal(barrier, inc=1, device_id={"head": me - 2}, device_id_type=MESH)

    @pl.when(chip < chips - 1)
    def _():
        pl.semaphore_signal(barrier, inc=1, device_id={"head": me + 2}, device_id_type=MESH)

    below = (chip + chips - 1) // chips
    above = (2 * chips - 2 - chip) // chips
    pl.semaphore_wait(barrier, 1 + below + above)


def gather_kernel(chips, x_ref, out_ref, own_sem, up_send, down_send, chip_recv, pair_send, pair_recv):
    me = lax.axis_index("head")
    chip = me // 2
    core = me % 2
    partner = chip * 2 + (1 - core)
    chain_barrier(chips, me, chip, partner)

    def to_up(src, owner):
        return pltpu.make_async_remote_copy(
            src_ref=src,
            dst_ref=out_ref.at[owner * 2 + core],
            send_sem=up_send.at[owner],
            recv_sem=chip_recv.at[owner],
            device_id={"head": me + 2},
            device_id_type=MESH,
        )

    def to_down(src, owner):
        return pltpu.make_async_remote_copy(
            src_ref=src,
            dst_ref=out_ref.at[owner * 2 + core],
            send_sem=down_send.at[owner],
            recv_sem=chip_recv.at[owner],
            device_id={"head": me - 2},
            device_id_type=MESH,
        )

    def to_partner(src, owner):
        return pltpu.make_async_remote_copy(
            src_ref=src,
            dst_ref=out_ref.at[owner * 2 + core],
            send_sem=pair_send.at[owner],
            recv_sem=pair_recv.at[owner],
            device_id={"head": partner},
            device_id_type=MESH,
        )

    @pl.when(chip < chips - 1)
    def _():
        to_up(x_ref, chip).start()

    @pl.when(chip > 0)
    def _():
        to_down(x_ref, chip).start()

    to_partner(x_ref, chip).start()
    own = pltpu.make_async_copy(x_ref, out_ref.at[me], own_sem)
    own.start()

    def step(s, carry):
        @pl.when(chip - s >= 0)
        def _():
            owner = chip - s
            held = out_ref.at[owner * 2 + core]
            to_up(held, owner).wait_recv()

            @pl.when(chip < chips - 1)
            def _():
                to_up(held, owner).start()

            to_partner(held, owner).start()

        @pl.when(chip + s <= chips - 1)
        def _():
            owner = chip + s
            held = out_ref.at[owner * 2 + core]
            to_down(held, owner).wait_recv()

            @pl.when(chip > 0)
            def _():
                to_down(held, owner).start()

            to_partner(held, owner).start()

        return carry

    lax.fori_loop(1, chips, step, 0)
    own.wait()

    def finish(owner, carry):
        to_partner(x_ref, owner).wait()

        @pl.when((chip < chips - 1) & (owner <= chip))
        def _():
            to_up(x_ref, owner).wait_send()

        @pl.when((chip > 0) & (owner >= chip))
        def _():
            to_down(x_ref, owner).wait_send()

        return carry

    lax.fori_loop(0, chips, finish, 0)


def gather(x, size, collective_id):
    chips = size // 2
    return pl.pallas_call(
        functools.partial(gather_kernel, chips),
        out_shape=jax.ShapeDtypeStruct((size,) + x.shape, x.dtype),
        in_specs=[pl.BlockSpec(memory_space=pl.ANY)],
        out_specs=pl.BlockSpec(memory_space=pl.ANY),
        scratch_shapes=[pltpu.SemaphoreType.DMA(())] + [pltpu.SemaphoreType.DMA((chips,))] * 5,
        compiler_params=pltpu.CompilerParams(collective_id=collective_id, has_side_effects=True),
        name="gather%d" % collective_id,
    )(x)


def scatter_kernel(
    chips, x_ref, out_ref, pair, up, down, pair_send, pair_recv, up_send, up_recv, down_send, down_recv
):
    me = lax.axis_index("head")
    chip = me // 2
    core = me % 2
    partner = chip * 2 + (1 - core)
    half = chip // (chips // 2)
    chain_barrier(chips, me, chip, partner)

    def to_partner(j):
        return pltpu.make_async_remote_copy(
            src_ref=x_ref.at[2 * j + (1 - core)],
            dst_ref=pair.at[j],
            send_sem=pair_send.at[j],
            recv_sem=pair_recv.at[j],
            device_id={"head": partner},
            device_id_type=MESH,
        )

    def to_up(src, j):
        return pltpu.make_async_remote_copy(
            src_ref=src,
            dst_ref=up.at[j],
            send_sem=up_send.at[j],
            recv_sem=up_recv.at[j],
            device_id={"head": me + 2},
            device_id_type=MESH,
        )

    def to_down(src, j):
        return pltpu.make_async_remote_copy(
            src_ref=src,
            dst_ref=down.at[j],
            send_sem=down_send.at[j],
            recv_sem=down_recv.at[j],
            device_id={"head": me - 2},
            device_id_type=MESH,
        )

    def order(k):
        return (1 - half) * (chips - 1 - k) + half * k

    def first(k, carry):
        to_partner(order(k)).start()
        return carry

    lax.fori_loop(0, chips, first, 0)

    def second(k, carry):
        j = order(k)
        to_partner(j).wait_recv()
        pair[j] = pair[j] + x_ref[2 * j + core]

        @pl.when((chip == 0) & (j > 0))
        def _():
            to_up(pair.at[j], j).start()

        @pl.when((chip == chips - 1) & (j < chips - 1))
        def _():
            to_down(pair.at[j], j).start()

        return carry

    lax.fori_loop(0, chips, second, 0)

    def move_up(j):
        @pl.when((chip > 0) & (j > chip))
        def _():
            to_up(up.at[j], j).wait_recv()
            up[j] = up[j] + pair[j]
            to_up(up.at[j], j).start()

    def move_down(j):
        @pl.when((chip < chips - 1) & (j < chip))
        def _():
            to_down(down.at[j], j).wait_recv()
            down[j] = down[j] + pair[j]
            to_down(down.at[j], j).start()

    def third(s, carry):
        @pl.when(half == 0)
        def _():
            move_up(chips - 1 - s)

        move_down(s)

        @pl.when(half == 1)
        def _():
            move_up(chips - 1 - s)

        return carry

    lax.fori_loop(0, chips - 1, third, 0)
    out_ref[...] = pair[chip].astype(jnp.float32)

    @pl.when(chip > 0)
    def _():
        to_up(up.at[chip], chip).wait_recv()
        out_ref[...] = out_ref[...] + up[chip].astype(jnp.float32)

    @pl.when(chip < chips - 1)
    def _():
        to_down(down.at[chip], chip).wait_recv()
        out_ref[...] = out_ref[...] + down[chip].astype(jnp.float32)

    def finish(j, carry):
        to_partner(j).wait_send()

        @pl.when(j > chip)
        def _():
            to_up(pair.at[j], j).wait_send()

        @pl.when(j < chip)
        def _():
            to_down(pair.at[j], j).wait_send()

        return carry

    lax.fori_loop(0, chips, finish, 0)


def scatter(x, size, collective_id):
    chips = size // 2
    shape = x.shape[1:]
    return pl.pallas_call(
        functools.partial(scatter_kernel, chips),
        out_shape=jax.ShapeDtypeStruct(shape, jnp.float32),
        in_specs=[pl.BlockSpec(memory_space=pltpu.VMEM)],
        out_specs=pl.BlockSpec(memory_space=pltpu.VMEM),
        scratch_shapes=[pltpu.VMEM((chips,) + shape, x.dtype)] * 3
        + [pltpu.SemaphoreType.DMA((chips,))] * 6,
        compiler_params=pltpu.CompilerParams(
            collective_id=collective_id, has_side_effects=True, vmem_limit_bytes=24 << 20
        ),
        name="scatter%d" % collective_id,
    )(x)


def factor_kernel(size, x_ref, out_ref, held, send_sem, recv_sem):
    me = lax.axis_index("head")
    barrier = pltpu.get_barrier_semaphore()

    def greet(k, carry):
        pl.semaphore_signal(
            barrier, inc=1, device_id={"head": (me + k) % size}, device_id_type=MESH
        )
        return carry

    lax.fori_loop(1, size, greet, 0)
    pl.semaphore_wait(barrier, size - 1)

    def copy(slot, other):
        return pltpu.make_async_remote_copy(
            src_ref=x_ref,
            dst_ref=held.at[slot],
            send_sem=send_sem.at[other],
            recv_sem=recv_sem.at[slot],
            device_id={"head": other},
            device_id_type=MESH,
        )

    def start(k, carry):
        copy(me, (me + k) % size).start()
        return carry

    lax.fori_loop(1, size, start, 0)

    def collect(k, best):
        other = (me + k) % size
        copy(other, other).wait_recv()
        return jnp.maximum(best, held[other])

    own = x_ref[...]
    best = lax.fori_loop(1, size, collect, own)
    out_ref[...] = jnp.exp((own - best) * SCALE)

    def finish(k, carry):
        copy(me, (me + k) % size).wait_send()
        return carry

    lax.fori_loop(1, size, finish, 0)


def joint_factor(x, size, collective_id):
    return pl.pallas_call(
        functools.partial(factor_kernel, size),
        out_shape=jax.ShapeDtypeStruct(x.shape, jnp.float32),
        in_specs=[pl.BlockSpec(memory_space=pltpu.VMEM)],
        out_specs=pl.BlockSpec(memory_space=pltpu.VMEM),
        scratch_shapes=[
            pltpu.VMEM((size,) + x.shape, x.dtype),
            pltpu.SemaphoreType.DMA((size,)),
            pltpu.SemaphoreType.DMA((size,)),
        ],
        compiler_params=pltpu.CompilerParams(collective_id=collective_id, has_side_effects=True),
        name="factor%d" % collective_id,
    )(x)


def attend_kernel(info_ref, q_ref, kc_ref, vc_ref, kn_ref, vn_ref, cos_ref, sin_ref, sum_ref, max_ref):
    tokens = q_ref.shape[0]
    length = kc_ref.shape[0]
    fresh = kn_ref.shape[0]
    width = GROUP * tokens
    cosine = cos_ref[...]
    sine = sin_ref[...]
    parts = []
    for j in range(GROUP):
        data = q_ref[:, j * HEAD_WIDTH : (j + 1) * HEAD_WIDTH].astype(jnp.float32)
        turned = pltpu.roll(data, HEAD_WIDTH // 2, 1)
        parts.append((data * cosine + turned * sine).astype(jnp.bfloat16))
    query = jnp.concatenate(parts, axis=0)
    last = (((1,), (1,)), ((), ()))
    first = (((0,), (0,)), ((), ()))
    old = lax.dot_general(kc_ref[...], query, last, preferred_element_type=jnp.float32)
    new = lax.dot_general(kn_ref[...], query, last, preferred_element_type=jnp.float32)
    old_ids = lax.broadcasted_iota(jnp.int32, (length, 1), 0)
    old = jnp.where(old_ids < info_ref[0], old, -1e30)
    new_ids = lax.broadcasted_iota(jnp.int32, (fresh, width), 0) + info_ref[1]
    token_ids = lax.broadcasted_iota(jnp.int32, (fresh, width), 1) % tokens
    new = jnp.where(new_ids <= token_ids, new, -1e30)
    top = jnp.maximum(jnp.max(old, axis=0, keepdims=True), jnp.max(new, axis=0, keepdims=True))
    top = jnp.maximum(top, -1e29)
    old = jnp.exp((old - top) * SCALE)
    new = jnp.exp((new - top) * SCALE)
    total = jnp.sum(old, axis=0, keepdims=True) + jnp.sum(new, axis=0, keepdims=True)
    sums = lax.dot_general(
        vc_ref[...], old.astype(jnp.bfloat16), first, preferred_element_type=jnp.float32
    ) + lax.dot_general(
        vn_ref[...], new.astype(jnp.bfloat16), first, preferred_element_type=jnp.float32
    )
    sum_ref[0, :HEAD_WIDTH, :] = sums.astype(jnp.bfloat16)
    sum_ref[0, HEAD_WIDTH:, :] = jnp.broadcast_to(total, (TAIL, width)).astype(jnp.bfloat16)
    max_ref[pl.ds(pl.program_id(0), 1), :] = top


def attend(info, qkv, key_cache, value_cache, new_keys, new_values, cosine, sine):
    tokens = qkv.shape[0]
    length = key_cache.shape[0]
    fresh = new_keys.shape[0]
    width = GROUP * tokens

    def head_block(rows):
        return pl.BlockSpec((rows, HEAD_WIDTH), lambda g, info: (0, g))

    def whole_block(shape):
        return pl.BlockSpec(shape, lambda g, info: (0, 0))

    return pl.pallas_call(
        attend_kernel,
        grid_spec=pltpu.PrefetchScalarGridSpec(
            num_scalar_prefetch=1,
            grid=(KEY_VALUE_HEADS,),
            in_specs=[
                pl.BlockSpec((tokens, GROUP * HEAD_WIDTH), lambda g, info: (0, g)),
                head_block(length),
                head_block(length),
                head_block(fresh),
                head_block(fresh),
                whole_block((tokens, HEAD_WIDTH)),
                whole_block((tokens, HEAD_WIDTH)),
            ],
            out_specs=[
                pl.BlockSpec((1, HEAD_WIDTH + TAIL, width), lambda g, info: (g, 0, 0)),
                whole_block((KEY_VALUE_HEADS, width)),
            ],
        ),
        out_shape=[
            jax.ShapeDtypeStruct((KEY_VALUE_HEADS, HEAD_WIDTH + TAIL, width), jnp.bfloat16),
            jax.ShapeDtypeStruct((KEY_VALUE_HEADS, width), jnp.float32),
        ],
        compiler_params=pltpu.CompilerParams(
            dimension_semantics=("arbitrary",), vmem_limit_bytes=32 << 20
        ),
        name="attend",
    )(info, qkv, key_cache, value_cache, new_keys, new_values, cosine, sine)


def on_device(
    hidden,
    cached_len,
    attn_gain,
    query_key_value_weight,
    b_qkv,
    key_cache,
    value_cache,
    w_out,
    ffn_gain,
    w_gate,
    w_up,
    w_down,
):
    size = lax.axis_size("head")
    index_here = lax.axis_index("head")
    own_rows = hidden[0]
    fresh, model = own_rows.shape
    tokens = fresh * size
    heads_here = QUERY_HEADS // size
    row_start = index_here * fresh
    cache_length = key_cache.shape[1]
    key_start = QUERY_HEADS * HEAD_WIDTH

    cosine, sine = rope_tables(cached_len[0] + jnp.arange(tokens, dtype=jnp.int32))
    own_cosine = lax.dynamic_slice_in_dim(cosine, row_start, fresh, 0)[:, None, :]
    own_sine = lax.dynamic_slice_in_dim(sine, row_start, fresh, 0)[:, None, :]

    normed = gather(rms_norm(own_rows, attn_gain), size, 0).reshape(tokens, model)
    qkv_part = (
        jnp.dot(normed, query_key_value_weight, preferred_element_type=jnp.float32)
        + b_qkv.astype(jnp.float32)
    ).astype(jnp.bfloat16)
    qkv = jnp.transpose(gather(qkv_part, size, 1), (1, 0, 2)).reshape(tokens, -1)
    own = lax.dynamic_slice(
        qkv, (row_start, key_start), (fresh, 2 * KEY_VALUE_HEADS * HEAD_WIDTH)
    )
    key_data = own[:, : KEY_VALUE_HEADS * HEAD_WIDTH].astype(jnp.float32)
    key_data = key_data.reshape(fresh, KEY_VALUE_HEADS, HEAD_WIDTH)
    turned = jnp.roll(key_data, HEAD_WIDTH // 2, axis=-1)
    new_keys = (key_data * own_cosine + turned * own_sine).astype(jnp.bfloat16)
    new_keys = new_keys.reshape(fresh, KEY_VALUE_HEADS * HEAD_WIDTH)
    new_values = own[:, KEY_VALUE_HEADS * HEAD_WIDTH :]

    info = jnp.stack([cached_len[0] - index_here * cache_length, row_start]).astype(jnp.int32)
    sums, tops = attend(
        info, qkv, key_cache[0], value_cache[0], new_keys, new_values, cosine, sine
    )
    factor = joint_factor(tops, size, 2)
    sums = (sums.astype(jnp.float32) * factor[:, None, :]).astype(jnp.bfloat16)
    split = size // KEY_VALUE_HEADS
    width = heads_here * tokens
    sums = jnp.transpose(
        sums.reshape(KEY_VALUE_HEADS, HEAD_WIDTH + TAIL, split, width), (0, 2, 1, 3)
    ).reshape(size, HEAD_WIDTH + TAIL, width)
    mixed = scatter(sums, size, 3)
    attn = (mixed[:HEAD_WIDTH] / mixed[HEAD_WIDTH : HEAD_WIDTH + 1]).astype(jnp.bfloat16)
    attn = jnp.transpose(attn.reshape(HEAD_WIDTH, heads_here, tokens), (2, 1, 0))
    attn = attn.reshape(tokens, heads_here * HEAD_WIDTH)
    projected = jnp.dot(attn, w_out, preferred_element_type=jnp.float32).astype(jnp.bfloat16)
    projected = scatter(projected.reshape(size, fresh, model), size, 4)
    middle = (own_rows.astype(jnp.float32) + projected).astype(jnp.bfloat16)
    normed_two = gather(rms_norm(middle, ffn_gain), size, 5).reshape(tokens, model)
    gate = jnp.dot(normed_two, w_gate, preferred_element_type=jnp.float32)
    upward = jnp.dot(normed_two, w_up, preferred_element_type=jnp.float32)
    active = (jax.nn.silu(gate) * upward).astype(jnp.bfloat16)
    active = lax.optimization_barrier(active)
    ffn_part = jnp.dot(active, w_down, preferred_element_type=jnp.float32).astype(jnp.bfloat16)
    ffn_sum = scatter(ffn_part.reshape(size, fresh, model), size, 6)
    result = (middle.astype(jnp.float32) + ffn_sum).astype(jnp.bfloat16)
    return (result[None], new_keys[None], new_values[None])


def solution(mesh):
    in_specs = (
        P("req", "head", None),
        P("req"),
        P(),
        P(None, "head"),
        P("head"),
        P("req", "head", None),
        P("req", "head", None),
        P("head", None),
        P(),
        P(None, "head"),
        P(None, "head"),
        P("head", None),
    )
    out_specs = (P("req", "head", None), P("req", "head", None), P("req", "head", None))
    return jax.shard_map(
        on_device, mesh=mesh, in_specs=in_specs, out_specs=out_specs, check_vma=False
    )
```

```python
import functools
import math

import jax
import jax.numpy as jnp
from jax import lax
from jax.experimental import pallas as pl
from jax.experimental.pallas import tpu as pltpu
from jax.sharding import PartitionSpec as P

QUERY_HEADS = 32
KEY_VALUE_HEADS = 8
HEAD_WIDTH = 128
GROUP = QUERY_HEADS // KEY_VALUE_HEADS
SCALE = 1.0 / math.sqrt(HEAD_WIDTH)
TAIL = 16
FEED_TILE = 432

rope_base = 1000000.0
MESH = pl.DeviceIdType.MESH


def rms_norm(values, gain):
    data = values.astype(jnp.float32)
    spread = jnp.mean(data * data, axis=-1, keepdims=True)
    return (data * lax.rsqrt(spread + 1e-06) * gain).astype(jnp.bfloat16)


def rope_tables(positions):
    half_dim = HEAD_WIDTH // 2
    inverse = rope_base ** (-(jnp.arange(half_dim, dtype=jnp.float32) * 2.0 / HEAD_WIDTH))
    angles = positions.astype(jnp.float32)[:, None] * inverse[None, :]
    cosine = jnp.cos(angles)
    sine = jnp.sin(angles)
    return (
        jnp.concatenate([cosine, cosine], axis=-1),
        jnp.concatenate([-sine, sine], axis=-1),
    )


def chain_barrier(chips, me, chip, partner):
    barrier = pltpu.get_barrier_semaphore()
    pl.semaphore_signal(barrier, inc=1, device_id={"head": partner}, device_id_type=MESH)

    @pl.when(chip > 0)
    def _():
        pl.semaphore_signal(barrier, inc=1, device_id={"head": me - 2}, device_id_type=MESH)

    @pl.when(chip < chips - 1)
    def _():
        pl.semaphore_signal(barrier, inc=1, device_id={"head": me + 2}, device_id_type=MESH)

    below = (chip + chips - 1) // chips
    above = (2 * chips - 2 - chip) // chips
    pl.semaphore_wait(barrier, 1 + below + above)


def gather_kernel(
    chips, pieces, x_ref, out_ref, own_sem, up_send, down_send, chip_recv, pair_send, pair_recv
):
    me = lax.axis_index("head")
    chip = me // 2
    core = me % 2
    partner = chip * 2 + (1 - core)
    chain_barrier(chips, me, chip, partner)

    def to_up(src, owner, c):
        return pltpu.make_async_remote_copy(
            src_ref=src,
            dst_ref=out_ref.at[owner * 2 + core, c],
            send_sem=up_send.at[owner, c],
            recv_sem=chip_recv.at[owner, c],
            device_id={"head": me + 2},
            device_id_type=MESH,
        )

    def to_down(src, owner, c):
        return pltpu.make_async_remote_copy(
            src_ref=src,
            dst_ref=out_ref.at[owner * 2 + core, c],
            send_sem=down_send.at[owner, c],
            recv_sem=chip_recv.at[owner, c],
            device_id={"head": me - 2},
            device_id_type=MESH,
        )

    def to_partner(src, owner, c):
        return pltpu.make_async_remote_copy(
            src_ref=src,
            dst_ref=out_ref.at[owner * 2 + core, c],
            send_sem=pair_send.at[owner, c],
            recv_sem=pair_recv.at[owner, c],
            device_id={"head": partner},
            device_id_type=MESH,
        )

    def begin(c, carry):
        @pl.when(chip < chips - 1)
        def _():
            to_up(x_ref.at[c], chip, c).start()

        @pl.when(chip > 0)
        def _():
            to_down(x_ref.at[c], chip, c).start()

        to_partner(x_ref.at[c], chip, c).start()
        return carry

    lax.fori_loop(0, pieces, begin, 0)
    own = pltpu.make_async_copy(x_ref, out_ref.at[me], own_sem)
    own.start()

    def step(t, carry):
        s = 1 + t // pieces
        c = t % pieces

        @pl.when(chip - s >= 0)
        def _():
            owner = chip - s
            held = out_ref.at[owner * 2 + core, c]
            to_up(held, owner, c).wait_recv()

            @pl.when(chip < chips - 1)
            def _():
                to_up(held, owner, c).start()

            to_partner(held, owner, c).start()

        @pl.when(chip + s <= chips - 1)
        def _():
            owner = chip + s
            held = out_ref.at[owner * 2 + core, c]
            to_down(held, owner, c).wait_recv()

            @pl.when(chip > 0)
            def _():
                to_down(held, owner, c).start()

            to_partner(held, owner, c).start()

        return carry

    lax.fori_loop(0, (chips - 1) * pieces, step, 0)
    own.wait()

    def finish(t, carry):
        owner = t // pieces
        c = t % pieces
        to_partner(x_ref.at[c], owner, c).wait()

        @pl.when((chip < chips - 1) & (owner <= chip))
        def _():
            to_up(x_ref.at[c], owner, c).wait_send()

        @pl.when((chip > 0) & (owner >= chip))
        def _():
            to_down(x_ref.at[c], owner, c).wait_send()

        return carry

    lax.fori_loop(0, chips * pieces, finish, 0)


def gather(x, size, pieces, collective_id):
    chips = size // 2
    rows, width = x.shape
    x = x.reshape(pieces, rows // pieces, width)
    return pl.pallas_call(
        functools.partial(gather_kernel, chips, pieces),
        out_shape=jax.ShapeDtypeStruct((size,) + x.shape, x.dtype),
        in_specs=[pl.BlockSpec(memory_space=pl.ANY)],
        out_specs=pl.BlockSpec(memory_space=pl.ANY),
        scratch_shapes=[pltpu.SemaphoreType.DMA(())]
        + [pltpu.SemaphoreType.DMA((chips, pieces))] * 5,
        compiler_params=pltpu.CompilerParams(collective_id=collective_id, has_side_effects=True),
        name="gather%d" % collective_id,
    )(x).reshape(size, rows, width)


def scatter_kernel(
    chips,
    pieces,
    x_ref,
    out_ref,
    pair,
    up,
    down,
    pair_send,
    pair_recv,
    up_send,
    up_recv,
    down_send,
    down_recv,
):
    me = lax.axis_index("head")
    chip = me // 2
    core = me % 2
    partner = chip * 2 + (1 - core)
    half = chip // (chips // 2)
    chain_barrier(chips, me, chip, partner)

    def to_partner(j, c):
        return pltpu.make_async_remote_copy(
            src_ref=x_ref.at[2 * j + (1 - core), c],
            dst_ref=pair.at[j, c],
            send_sem=pair_send.at[j, c],
            recv_sem=pair_recv.at[j, c],
            device_id={"head": partner},
            device_id_type=MESH,
        )

    def to_up(src, j, c):
        return pltpu.make_async_remote_copy(
            src_ref=src.at[j, c],
            dst_ref=up.at[j, c],
            send_sem=up_send.at[j, c],
            recv_sem=up_recv.at[j, c],
            device_id={"head": me + 2},
            device_id_type=MESH,
        )

    def to_down(src, j, c):
        return pltpu.make_async_remote_copy(
            src_ref=src.at[j, c],
            dst_ref=down.at[j, c],
            send_sem=down_send.at[j, c],
            recv_sem=down_recv.at[j, c],
            device_id={"head": me - 2},
            device_id_type=MESH,
        )

    def order(k):
        return (1 - half) * (chips - 1 - k) + half * k

    def first(t, carry):
        to_partner(order(t // pieces), t % pieces).start()
        return carry

    lax.fori_loop(0, chips * pieces, first, 0)

    def second(t, carry):
        j = order(t // pieces)
        c = t % pieces
        to_partner(j, c).wait_recv()
        pair[j, c] = pair[j, c] + x_ref[2 * j + core, c]

        @pl.when((chip == 0) & (j > 0))
        def _():
            to_up(pair, j, c).start()

        @pl.when((chip == chips - 1) & (j < chips - 1))
        def _():
            to_down(pair, j, c).start()

        return carry

    lax.fori_loop(0, chips * pieces, second, 0)

    def move_up(j, c):
        @pl.when((chip > 0) & (j > chip))
        def _():
            to_up(up, j, c).wait_recv()
            up[j, c] = up[j, c] + pair[j, c]
            to_up(up, j, c).start()

    def move_down(j, c):
        @pl.when((chip < chips - 1) & (j < chip))
        def _():
            to_down(down, j, c).wait_recv()
            down[j, c] = down[j, c] + pair[j, c]
            to_down(down, j, c).start()

    def third(t, carry):
        s = t // pieces
        c = t % pieces

        @pl.when(half == 0)
        def _():
            move_up(chips - 1 - s, c)

        move_down(s, c)

        @pl.when(half == 1)
        def _():
            move_up(chips - 1 - s, c)

        return carry

    lax.fori_loop(0, (chips - 1) * pieces, third, 0)

    def total(c, carry):
        out_ref[c] = pair[chip, c].astype(jnp.float32)

        @pl.when(chip > 0)
        def _():
            to_up(up, chip, c).wait_recv()
            out_ref[c] = out_ref[c] + up[chip, c].astype(jnp.float32)

        @pl.when(chip < chips - 1)
        def _():
            to_down(down, chip, c).wait_recv()
            out_ref[c] = out_ref[c] + down[chip, c].astype(jnp.float32)

        return carry

    lax.fori_loop(0, pieces, total, 0)

    def finish(t, carry):
        j = t // pieces
        c = t % pieces
        to_partner(j, c).wait_send()

        @pl.when(j > chip)
        def _():
            to_up(pair, j, c).wait_send()

        @pl.when(j < chip)
        def _():
            to_down(pair, j, c).wait_send()

        return carry

    lax.fori_loop(0, chips * pieces, finish, 0)


def scatter(x, size, pieces, collective_id):
    chips = size // 2
    rows, width = x.shape[1:]
    shape = (pieces, rows // pieces, width)
    return pl.pallas_call(
        functools.partial(scatter_kernel, chips, pieces),
        out_shape=jax.ShapeDtypeStruct(shape, jnp.float32),
        in_specs=[pl.BlockSpec(memory_space=pltpu.VMEM)],
        out_specs=pl.BlockSpec(memory_space=pltpu.VMEM),
        scratch_shapes=[pltpu.VMEM((chips,) + shape, x.dtype)] * 3
        + [pltpu.SemaphoreType.DMA((chips, pieces))] * 6,
        compiler_params=pltpu.CompilerParams(
            collective_id=collective_id, has_side_effects=True, vmem_limit_bytes=24 << 20
        ),
        name="scatter%d" % collective_id,
    )(x.reshape((size,) + shape)).reshape(rows, width)


def factor_kernel(size, x_ref, out_ref, held, send_sem, recv_sem):
    me = lax.axis_index("head")
    barrier = pltpu.get_barrier_semaphore()

    def greet(k, carry):
        pl.semaphore_signal(
            barrier, inc=1, device_id={"head": (me + k) % size}, device_id_type=MESH
        )
        return carry

    lax.fori_loop(1, size, greet, 0)
    pl.semaphore_wait(barrier, size - 1)

    def copy(slot, other):
        return pltpu.make_async_remote_copy(
            src_ref=x_ref,
            dst_ref=held.at[slot],
            send_sem=send_sem.at[other],
            recv_sem=recv_sem.at[slot],
            device_id={"head": other},
            device_id_type=MESH,
        )

    def start(k, carry):
        copy(me, (me + k) % size).start()
        return carry

    lax.fori_loop(1, size, start, 0)

    def collect(k, best):
        other = (me + k) % size
        copy(other, other).wait_recv()
        return jnp.maximum(best, held[other])

    own = x_ref[...]
    best = lax.fori_loop(1, size, collect, own)
    out_ref[...] = jnp.exp((own - best) * SCALE)

    def finish(k, carry):
        copy(me, (me + k) % size).wait_send()
        return carry

    lax.fori_loop(1, size, finish, 0)


def joint_factor(x, size, collective_id):
    return pl.pallas_call(
        functools.partial(factor_kernel, size),
        out_shape=jax.ShapeDtypeStruct(x.shape, jnp.float32),
        in_specs=[pl.BlockSpec(memory_space=pltpu.VMEM)],
        out_specs=pl.BlockSpec(memory_space=pltpu.VMEM),
        scratch_shapes=[
            pltpu.VMEM((size,) + x.shape, x.dtype),
            pltpu.SemaphoreType.DMA((size,)),
            pltpu.SemaphoreType.DMA((size,)),
        ],
        compiler_params=pltpu.CompilerParams(collective_id=collective_id, has_side_effects=True),
        name="factor%d" % collective_id,
    )(x)


def attend_kernel(info_ref, q_ref, kc_ref, vc_ref, kn_ref, vn_ref, cos_ref, sin_ref, sum_ref, max_ref):
    tokens = q_ref.shape[0]
    length = kc_ref.shape[0]
    fresh = kn_ref.shape[0]
    width = GROUP * tokens
    cosine = cos_ref[...]
    sine = sin_ref[...]
    parts = []
    for j in range(GROUP):
        data = q_ref[:, j * HEAD_WIDTH : (j + 1) * HEAD_WIDTH].astype(jnp.float32)
        turned = pltpu.roll(data, HEAD_WIDTH // 2, 1)
        parts.append((data * cosine + turned * sine).astype(jnp.bfloat16))
    query = jnp.concatenate(parts, axis=0)
    last = (((1,), (1,)), ((), ()))
    first = (((0,), (0,)), ((), ()))
    old = lax.dot_general(kc_ref[...], query, last, preferred_element_type=jnp.float32)
    new = lax.dot_general(kn_ref[...], query, last, preferred_element_type=jnp.float32)
    old_ids = lax.broadcasted_iota(jnp.int32, (length, 1), 0)
    old = jnp.where(old_ids < info_ref[0], old, -1e30)
    new_ids = lax.broadcasted_iota(jnp.int32, (fresh, width), 0) + info_ref[1]
    token_ids = lax.broadcasted_iota(jnp.int32, (fresh, width), 1) % tokens
    new = jnp.where(new_ids <= token_ids, new, -1e30)
    top = jnp.maximum(jnp.max(old, axis=0, keepdims=True), jnp.max(new, axis=0, keepdims=True))
    top = jnp.maximum(top, -1e29)
    old = jnp.exp((old - top) * SCALE)
    new = jnp.exp((new - top) * SCALE)
    total = jnp.sum(old, axis=0, keepdims=True) + jnp.sum(new, axis=0, keepdims=True)
    sums = lax.dot_general(
        vc_ref[...], old.astype(jnp.bfloat16), first, preferred_element_type=jnp.float32
    ) + lax.dot_general(
        vn_ref[...], new.astype(jnp.bfloat16), first, preferred_element_type=jnp.float32
    )
    sum_ref[0, :HEAD_WIDTH, :] = sums.astype(jnp.bfloat16)
    sum_ref[0, HEAD_WIDTH:, :] = jnp.broadcast_to(total, (TAIL, width)).astype(jnp.bfloat16)
    max_ref[pl.ds(pl.program_id(0), 1), :] = top


def attend(info, qkv, key_cache, value_cache, new_keys, new_values, cosine, sine):
    tokens = qkv.shape[0]
    length = key_cache.shape[0]
    fresh = new_keys.shape[0]
    width = GROUP * tokens

    def head_block(rows):
        return pl.BlockSpec((rows, HEAD_WIDTH), lambda g, info: (0, g))

    def whole_block(shape):
        return pl.BlockSpec(shape, lambda g, info: (0, 0))

    return pl.pallas_call(
        attend_kernel,
        grid_spec=pltpu.PrefetchScalarGridSpec(
            num_scalar_prefetch=1,
            grid=(KEY_VALUE_HEADS,),
            in_specs=[
                pl.BlockSpec((tokens, GROUP * HEAD_WIDTH), lambda g, info: (0, g)),
                head_block(length),
                head_block(length),
                head_block(fresh),
                head_block(fresh),
                whole_block((tokens, HEAD_WIDTH)),
                whole_block((tokens, HEAD_WIDTH)),
            ],
            out_specs=[
                pl.BlockSpec((1, HEAD_WIDTH + TAIL, width), lambda g, info: (g, 0, 0)),
                whole_block((KEY_VALUE_HEADS, width)),
            ],
        ),
        out_shape=[
            jax.ShapeDtypeStruct((KEY_VALUE_HEADS, HEAD_WIDTH + TAIL, width), jnp.bfloat16),
            jax.ShapeDtypeStruct((KEY_VALUE_HEADS, width), jnp.float32),
        ],
        compiler_params=pltpu.CompilerParams(
            dimension_semantics=("arbitrary",), vmem_limit_bytes=32 << 20
        ),
        name="attend",
    )(info, qkv, key_cache, value_cache, new_keys, new_values, cosine, sine)


def feed_kernel(x_ref, gate_ref, up_ref, down_ref, out_ref, total):
    step = pl.program_id(0)
    last = (((1,), (1,)), ((), ()))
    first = (((0,), (0,)), ((), ()))
    x = x_ref[...]
    gate = lax.dot_general(gate_ref[...], x, last, preferred_element_type=jnp.float32)
    upward = lax.dot_general(up_ref[...], x, last, preferred_element_type=jnp.float32)
    active = (gate / (1.0 + jnp.exp(-gate)) * upward).astype(jnp.bfloat16)
    part = lax.dot_general(active, down_ref[...], first, preferred_element_type=jnp.float32)

    @pl.when(step == 0)
    def _():
        total[...] = part

    @pl.when(step > 0)
    def _():
        total[...] = total[...] + part

    @pl.when(step == pl.num_programs(0) - 1)
    def _():
        out_ref[...] = total[...].astype(jnp.bfloat16)


def feed(x, w_gate, w_up, w_down):
    tokens, model = x.shape
    units = w_down.shape[0]
    steps = units // FEED_TILE
    tile = units // steps
    weight = pl.BlockSpec((tile, model), lambda i: (i, 0))
    whole = pl.BlockSpec((tokens, model), lambda i: (0, 0))
    return pl.pallas_call(
        feed_kernel,
        grid=(steps,),
        in_specs=[whole, weight, weight, weight],
        out_specs=whole,
        out_shape=jax.ShapeDtypeStruct((tokens, model), jnp.bfloat16),
        scratch_shapes=[pltpu.VMEM((tokens, model), jnp.float32)],
        compiler_params=pltpu.CompilerParams(
            dimension_semantics=("arbitrary",), vmem_limit_bytes=56 << 20
        ),
        name="feed",
    )(x, jnp.transpose(w_gate), jnp.transpose(w_up), w_down)


def on_device(
    hidden,
    cached_len,
    attn_gain,
    query_key_value_weight,
    b_qkv,
    key_cache,
    value_cache,
    w_out,
    ffn_gain,
    w_gate,
    w_up,
    w_down,
):
    size = lax.axis_size("head")
    index_here = lax.axis_index("head")
    own_rows = hidden[0]
    fresh, model = own_rows.shape
    tokens = fresh * size
    heads_here = QUERY_HEADS // size
    row_start = index_here * fresh
    cache_length = key_cache.shape[1]
    key_start = QUERY_HEADS * HEAD_WIDTH
    fine = max(fresh // 8, 1)
    coarse = max(fresh // 16, 1)

    cosine, sine = rope_tables(cached_len[0] + jnp.arange(tokens, dtype=jnp.int32))
    own_cosine = lax.dynamic_slice_in_dim(cosine, row_start, fresh, 0)[:, None, :]
    own_sine = lax.dynamic_slice_in_dim(sine, row_start, fresh, 0)[:, None, :]

    normed = gather(rms_norm(own_rows, attn_gain), size, fine, 0).reshape(tokens, model)
    qkv_part = (
        jnp.dot(normed, query_key_value_weight, preferred_element_type=jnp.float32)
        + b_qkv.astype(jnp.float32)
    ).astype(jnp.bfloat16)
    qkv = jnp.transpose(gather(qkv_part, size, 4, 1), (1, 0, 2)).reshape(tokens, -1)
    own = lax.dynamic_slice(
        qkv, (row_start, key_start), (fresh, 2 * KEY_VALUE_HEADS * HEAD_WIDTH)
    )
    key_data = own[:, : KEY_VALUE_HEADS * HEAD_WIDTH].astype(jnp.float32)
    key_data = key_data.reshape(fresh, KEY_VALUE_HEADS, HEAD_WIDTH)
    turned = jnp.roll(key_data, HEAD_WIDTH // 2, axis=-1)
    new_keys = (key_data * own_cosine + turned * own_sine).astype(jnp.bfloat16)
    new_keys = new_keys.reshape(fresh, KEY_VALUE_HEADS * HEAD_WIDTH)
    new_values = own[:, KEY_VALUE_HEADS * HEAD_WIDTH :]

    info = jnp.stack([cached_len[0] - index_here * cache_length, row_start]).astype(jnp.int32)
    sums, tops = attend(
        info, qkv, key_cache[0], value_cache[0], new_keys, new_values, cosine, sine
    )
    factor = joint_factor(tops, size, 2)
    sums = (sums.astype(jnp.float32) * factor[:, None, :]).astype(jnp.bfloat16)
    split = size // KEY_VALUE_HEADS
    width = heads_here * tokens
    sums = jnp.transpose(
        sums.reshape(KEY_VALUE_HEADS, HEAD_WIDTH + TAIL, split, width), (0, 2, 1, 3)
    ).reshape(size, HEAD_WIDTH + TAIL, width)
    mixed = scatter(sums, size, 3, 3)
    attn = (mixed[:HEAD_WIDTH] / mixed[HEAD_WIDTH : HEAD_WIDTH + 1]).astype(jnp.bfloat16)
    attn = jnp.transpose(attn.reshape(HEAD_WIDTH, heads_here, tokens), (2, 1, 0))
    attn = attn.reshape(tokens, heads_here * HEAD_WIDTH)
    projected = jnp.dot(attn, w_out, preferred_element_type=jnp.float32).astype(jnp.bfloat16)
    projected = scatter(projected.reshape(size, fresh, model), size, coarse, 4)
    middle = (own_rows.astype(jnp.float32) + projected).astype(jnp.bfloat16)
    normed_two = gather(rms_norm(middle, ffn_gain), size, fine, 5).reshape(tokens, model)
    ffn_part = feed(normed_two, w_gate, w_up, w_down)
    ffn_sum = scatter(ffn_part.reshape(size, fresh, model), size, coarse, 6)
    result = (middle.astype(jnp.float32) + ffn_sum).astype(jnp.bfloat16)
    return (result[None], new_keys[None], new_values[None])


def solution(mesh):
    in_specs = (
        P("req", "head", None),
        P("req"),
        P(),
        P(None, "head"),
        P("head"),
        P("req", "head", None),
        P("req", "head", None),
        P("head", None),
        P(),
        P(None, "head"),
        P(None, "head"),
        P("head", None),
    )
    out_specs = (P("req", "head", None), P("req", "head", None), P("req", "head", None))
    return jax.shard_map(
        on_device, mesh=mesh, in_specs=in_specs, out_specs=out_specs, check_vma=False
    )
```

```python
import functools
import math

import jax
import jax.numpy as jnp
from jax import lax
from jax.experimental import pallas as pl
from jax.experimental.pallas import tpu as pltpu
from jax.sharding import PartitionSpec as P

QUERY_HEADS = 32
KEY_VALUE_HEADS = 8
HEAD_WIDTH = 128
GROUP = QUERY_HEADS // KEY_VALUE_HEADS
SCALE = 1.0 / math.sqrt(HEAD_WIDTH)
TAIL = 16
FEED_TILE = 432
FEED_COLUMNS = 1024

rope_base = 1000000.0
MESH = pl.DeviceIdType.MESH


def rms_norm(values, gain):
    data = values.astype(jnp.float32)
    spread = jnp.mean(data * data, axis=-1, keepdims=True)
    return (data * lax.rsqrt(spread + 1e-06) * gain).astype(jnp.bfloat16)


def rope_tables(positions):
    half_dim = HEAD_WIDTH // 2
    inverse = rope_base ** (-(jnp.arange(half_dim, dtype=jnp.float32) * 2.0 / HEAD_WIDTH))
    angles = positions.astype(jnp.float32)[:, None] * inverse[None, :]
    cosine = jnp.cos(angles)
    sine = jnp.sin(angles)
    return (
        jnp.concatenate([cosine, cosine], axis=-1),
        jnp.concatenate([-sine, sine], axis=-1),
    )


def chain_barrier(chips, me, chip, partner):
    barrier = pltpu.get_barrier_semaphore()
    pl.semaphore_signal(barrier, inc=1, device_id={"head": partner}, device_id_type=MESH)

    @pl.when(chip > 0)
    def _():
        pl.semaphore_signal(barrier, inc=1, device_id={"head": me - 2}, device_id_type=MESH)

    @pl.when(chip < chips - 1)
    def _():
        pl.semaphore_signal(barrier, inc=1, device_id={"head": me + 2}, device_id_type=MESH)

    below = (chip + chips - 1) // chips
    above = (2 * chips - 2 - chip) // chips
    pl.semaphore_wait(barrier, 1 + below + above)


def gather_kernel(
    chips, pieces, x_ref, out_ref, own_sem, up_send, down_send, chip_recv, pair_send, pair_recv
):
    me = lax.axis_index("head")
    chip = me // 2
    core = me % 2
    partner = chip * 2 + (1 - core)
    chain_barrier(chips, me, chip, partner)

    def to_up(src, owner, c):
        return pltpu.make_async_remote_copy(
            src_ref=src,
            dst_ref=out_ref.at[owner * 2 + core, c],
            send_sem=up_send.at[owner, c],
            recv_sem=chip_recv.at[owner, c],
            device_id={"head": me + 2},
            device_id_type=MESH,
        )

    def to_down(src, owner, c):
        return pltpu.make_async_remote_copy(
            src_ref=src,
            dst_ref=out_ref.at[owner * 2 + core, c],
            send_sem=down_send.at[owner, c],
            recv_sem=chip_recv.at[owner, c],
            device_id={"head": me - 2},
            device_id_type=MESH,
        )

    def to_partner(src, owner, c):
        return pltpu.make_async_remote_copy(
            src_ref=src,
            dst_ref=out_ref.at[owner * 2 + core, c],
            send_sem=pair_send.at[owner, c],
            recv_sem=pair_recv.at[owner, c],
            device_id={"head": partner},
            device_id_type=MESH,
        )

    def begin(c, carry):
        @pl.when(chip < chips - 1)
        def _():
            to_up(x_ref.at[c], chip, c).start()

        @pl.when(chip > 0)
        def _():
            to_down(x_ref.at[c], chip, c).start()

        to_partner(x_ref.at[c], chip, c).start()
        return carry

    lax.fori_loop(0, pieces, begin, 0)
    own = pltpu.make_async_copy(x_ref, out_ref.at[me], own_sem)
    own.start()

    def step(t, carry):
        s = 1 + t // pieces
        c = t % pieces

        @pl.when(chip - s >= 0)
        def _():
            owner = chip - s
            held = out_ref.at[owner * 2 + core, c]
            to_up(held, owner, c).wait_recv()

            @pl.when(chip < chips - 1)
            def _():
                to_up(held, owner, c).start()

            to_partner(held, owner, c).start()

        @pl.when(chip + s <= chips - 1)
        def _():
            owner = chip + s
            held = out_ref.at[owner * 2 + core, c]
            to_down(held, owner, c).wait_recv()

            @pl.when(chip > 0)
            def _():
                to_down(held, owner, c).start()

            to_partner(held, owner, c).start()

        return carry

    lax.fori_loop(0, (chips - 1) * pieces, step, 0)
    own.wait()

    def finish(t, carry):
        owner = t // pieces
        c = t % pieces
        to_partner(x_ref.at[c], owner, c).wait()

        @pl.when((chip < chips - 1) & (owner <= chip))
        def _():
            to_up(x_ref.at[c], owner, c).wait_send()

        @pl.when((chip > 0) & (owner >= chip))
        def _():
            to_down(x_ref.at[c], owner, c).wait_send()

        return carry

    lax.fori_loop(0, chips * pieces, finish, 0)


def gather(x, size, pieces, collective_id):
    chips = size // 2
    rows, width = x.shape
    x = x.reshape(pieces, rows // pieces, width)
    return pl.pallas_call(
        functools.partial(gather_kernel, chips, pieces),
        out_shape=jax.ShapeDtypeStruct((size,) + x.shape, x.dtype),
        in_specs=[pl.BlockSpec(memory_space=pltpu.VMEM)],
        out_specs=pl.BlockSpec(memory_space=pltpu.VMEM),
        scratch_shapes=[pltpu.SemaphoreType.DMA(())]
        + [pltpu.SemaphoreType.DMA((chips, pieces))] * 5,
        compiler_params=pltpu.CompilerParams(
            collective_id=collective_id, has_side_effects=True, vmem_limit_bytes=16 << 20
        ),
        name="gather%d" % collective_id,
    )(x).reshape(size, rows, width)


def add_blocks(a, b):
    return a.astype(jnp.float32) + b.astype(jnp.float32)


def pack_sums(sums, total, top):
    def narrow(v):
        return v.astype(jnp.bfloat16).astype(jnp.float32)

    total_high = narrow(total)
    top_high = narrow(top)
    top_middle = narrow(top - top_high)
    rows = [total_high, total - total_high, top_high, top_middle, top - top_high - top_middle]
    index = lax.broadcasted_iota(jnp.int32, (TAIL, sums.shape[1]), 0)
    tail = jnp.zeros((TAIL, sums.shape[1]), jnp.float32)
    for place, row in enumerate(rows):
        tail = jnp.where(index == place, row, tail)
    return jnp.concatenate([sums, tail], axis=0)


def join_sums(a, b):
    def unpack(block):
        block = block.astype(jnp.float32)
        tail = block[HEAD_WIDTH:]
        return block[:HEAD_WIDTH], tail[0:1] + tail[1:2], (tail[2:3] + tail[3:4]) + tail[4:5]

    sums_a, total_a, top_a = unpack(a)
    sums_b, total_b, top_b = unpack(b)
    top = jnp.maximum(top_a, top_b)
    scale_a = jnp.exp((top_a - top) * SCALE)
    scale_b = jnp.exp((top_b - top) * SCALE)
    return pack_sums(
        sums_a * scale_a + sums_b * scale_b, total_a * scale_a + total_b * scale_b, top
    )


def scatter_kernel(
    join,
    chips,
    pieces,
    x_ref,
    out_ref,
    pair,
    up,
    down,
    pair_send,
    pair_recv,
    up_send,
    up_recv,
    down_send,
    down_recv,
):
    me = lax.axis_index("head")
    chip = me // 2
    core = me % 2
    partner = chip * 2 + (1 - core)
    half = chip // (chips // 2)
    chain_barrier(chips, me, chip, partner)

    def to_partner(j, c):
        return pltpu.make_async_remote_copy(
            src_ref=x_ref.at[2 * j + (1 - core), c],
            dst_ref=pair.at[j, c],
            send_sem=pair_send.at[j, c],
            recv_sem=pair_recv.at[j, c],
            device_id={"head": partner},
            device_id_type=MESH,
        )

    def to_up(src, j, c):
        return pltpu.make_async_remote_copy(
            src_ref=src.at[j, c],
            dst_ref=up.at[j, c],
            send_sem=up_send.at[j, c],
            recv_sem=up_recv.at[j, c],
            device_id={"head": me + 2},
            device_id_type=MESH,
        )

    def to_down(src, j, c):
        return pltpu.make_async_remote_copy(
            src_ref=src.at[j, c],
            dst_ref=down.at[j, c],
            send_sem=down_send.at[j, c],
            recv_sem=down_recv.at[j, c],
            device_id={"head": me - 2},
            device_id_type=MESH,
        )

    def order(k):
        return (1 - half) * (chips - 1 - k) + half * k

    def first(t, carry):
        to_partner(order(t // pieces), t % pieces).start()
        return carry

    lax.fori_loop(0, chips * pieces, first, 0)

    def second(t, carry):
        j = order(t // pieces)
        c = t % pieces
        to_partner(j, c).wait_recv()
        pair[j, c] = join(pair[j, c], x_ref[2 * j + core, c]).astype(pair.dtype)

        @pl.when((chip == 0) & (j > 0))
        def _():
            to_up(pair, j, c).start()

        @pl.when((chip == chips - 1) & (j < chips - 1))
        def _():
            to_down(pair, j, c).start()

        return carry

    lax.fori_loop(0, chips * pieces, second, 0)

    def move_up(j, c):
        @pl.when((chip > 0) & (j > chip))
        def _():
            to_up(up, j, c).wait_recv()
            up[j, c] = join(up[j, c], pair[j, c]).astype(up.dtype)
            to_up(up, j, c).start()

    def move_down(j, c):
        @pl.when((chip < chips - 1) & (j < chip))
        def _():
            to_down(down, j, c).wait_recv()
            down[j, c] = join(down[j, c], pair[j, c]).astype(down.dtype)
            to_down(down, j, c).start()

    def third(t, carry):
        s = t // pieces
        c = t % pieces

        @pl.when(half == 0)
        def _():
            move_up(chips - 1 - s, c)

        move_down(s, c)

        @pl.when(half == 1)
        def _():
            move_up(chips - 1 - s, c)

        return carry

    lax.fori_loop(0, (chips - 1) * pieces, third, 0)

    def total(c, carry):
        out_ref[c] = pair[chip, c].astype(jnp.float32)

        @pl.when(chip > 0)
        def _():
            to_up(up, chip, c).wait_recv()
            out_ref[c] = join(out_ref[c], up[chip, c])

        @pl.when(chip < chips - 1)
        def _():
            to_down(down, chip, c).wait_recv()
            out_ref[c] = join(out_ref[c], down[chip, c])

        return carry

    lax.fori_loop(0, pieces, total, 0)

    def finish(t, carry):
        j = t // pieces
        c = t % pieces
        to_partner(j, c).wait_send()

        @pl.when(j > chip)
        def _():
            to_up(pair, j, c).wait_send()

        @pl.when(j < chip)
        def _():
            to_down(pair, j, c).wait_send()

        return carry

    lax.fori_loop(0, chips * pieces, finish, 0)


def scatter(x, size, join, collective_id):
    chips = size // 2
    shape = x.shape[1:]
    pieces = shape[0]
    return pl.pallas_call(
        functools.partial(scatter_kernel, join, chips, pieces),
        out_shape=jax.ShapeDtypeStruct(shape, jnp.float32),
        in_specs=[pl.BlockSpec(memory_space=pltpu.VMEM)],
        out_specs=pl.BlockSpec(memory_space=pltpu.VMEM),
        scratch_shapes=[pltpu.VMEM((chips,) + shape, x.dtype)] * 3
        + [pltpu.SemaphoreType.DMA((chips, pieces))] * 6,
        compiler_params=pltpu.CompilerParams(
            collective_id=collective_id, has_side_effects=True, vmem_limit_bytes=24 << 20
        ),
        name="scatter%d" % collective_id,
    )(x)


def attend_kernel(info_ref, q_ref, kc_ref, vc_ref, kn_ref, vn_ref, cos_ref, sin_ref, sum_ref):
    tokens = q_ref.shape[0]
    length = kc_ref.shape[0]
    fresh = kn_ref.shape[0]
    width = GROUP * tokens
    cosine = cos_ref[...]
    sine = sin_ref[...]
    parts = []
    for j in range(GROUP):
        data = q_ref[:, j * HEAD_WIDTH : (j + 1) * HEAD_WIDTH].astype(jnp.float32)
        turned = pltpu.roll(data, HEAD_WIDTH // 2, 1)
        parts.append((data * cosine + turned * sine).astype(jnp.bfloat16))
    query = jnp.concatenate(parts, axis=0)
    last = (((1,), (1,)), ((), ()))
    first = (((0,), (0,)), ((), ()))
    old = lax.dot_general(kc_ref[...], query, last, preferred_element_type=jnp.float32)
    new = lax.dot_general(kn_ref[...], query, last, preferred_element_type=jnp.float32)
    old_ids = lax.broadcasted_iota(jnp.int32, (length, 1), 0)
    old = jnp.where(old_ids < info_ref[0], old, -1e30)
    new_ids = lax.broadcasted_iota(jnp.int32, (fresh, width), 0) + info_ref[1]
    token_ids = lax.broadcasted_iota(jnp.int32, (fresh, width), 1) % tokens
    new = jnp.where(new_ids <= token_ids, new, -1e30)
    top = jnp.maximum(jnp.max(old, axis=0, keepdims=True), jnp.max(new, axis=0, keepdims=True))
    top = jnp.maximum(top, -1e29)
    old = jnp.exp((old - top) * SCALE)
    new = jnp.exp((new - top) * SCALE)
    total = jnp.sum(old, axis=0, keepdims=True) + jnp.sum(new, axis=0, keepdims=True)
    sums = lax.dot_general(
        vc_ref[...], old.astype(jnp.bfloat16), first, preferred_element_type=jnp.float32
    ) + lax.dot_general(
        vn_ref[...], new.astype(jnp.bfloat16), first, preferred_element_type=jnp.float32
    )
    packed = pack_sums(sums, total, top).astype(jnp.bfloat16)
    for j in range(GROUP):
        sum_ref[0, j] = packed[:, j * tokens : (j + 1) * tokens]


def attend(info, qkv, key_cache, value_cache, new_keys, new_values, cosine, sine):
    tokens = qkv.shape[0]
    length = key_cache.shape[0]
    fresh = new_keys.shape[0]

    def head_block(rows):
        return pl.BlockSpec((rows, HEAD_WIDTH), lambda g, info: (0, g))

    def whole_block(shape):
        return pl.BlockSpec(shape, lambda g, info: (0, 0))

    return pl.pallas_call(
        attend_kernel,
        grid_spec=pltpu.PrefetchScalarGridSpec(
            num_scalar_prefetch=1,
            grid=(KEY_VALUE_HEADS,),
            in_specs=[
                pl.BlockSpec((tokens, GROUP * HEAD_WIDTH), lambda g, info: (0, g)),
                head_block(length),
                head_block(length),
                head_block(fresh),
                head_block(fresh),
                whole_block((tokens, HEAD_WIDTH)),
                whole_block((tokens, HEAD_WIDTH)),
            ],
            out_specs=pl.BlockSpec(
                (1, GROUP, HEAD_WIDTH + TAIL, tokens), lambda g, info: (g, 0, 0, 0)
            ),
        ),
        out_shape=jax.ShapeDtypeStruct(
            (KEY_VALUE_HEADS, GROUP, HEAD_WIDTH + TAIL, tokens), jnp.bfloat16
        ),
        compiler_params=pltpu.CompilerParams(
            dimension_semantics=("arbitrary",), vmem_limit_bytes=32 << 20
        ),
        name="attend",
    )(info, qkv, key_cache, value_cache, new_keys, new_values, cosine, sine)


def feed_kernel(steps, x_ref, gate_ref, up_ref, down_ref, out_ref, turned, active):
    step = pl.program_id(0)
    tile = gate_ref.shape[0]

    @pl.when(step == 0)
    def _():
        turned[...] = jnp.transpose(x_ref[...])

    @pl.when(step < steps)
    def _():
        x = turned[...]
        gate = jnp.dot(gate_ref[...], x, preferred_element_type=jnp.float32)
        upward = jnp.dot(up_ref[...], x, preferred_element_type=jnp.float32)
        active[pl.ds(pl.multiple_of(step * tile, tile), tile), :] = (
            gate / (1.0 + jnp.exp(-gate)) * upward
        ).astype(jnp.bfloat16)

    @pl.when(step >= steps)
    def _():
        out_ref[...] = lax.dot_general(
            active[...],
            down_ref[...],
            (((0,), (0,)), ((), ())),
            preferred_element_type=jnp.float32,
        ).astype(jnp.bfloat16)


def feed(x, w_gate, w_up, w_down):
    tokens, model = x.shape
    units = w_down.shape[0]
    steps = units // FEED_TILE
    tile = units // steps
    weight = pl.BlockSpec((tile, model), lambda i: (jnp.minimum(i, steps - 1), 0))
    return pl.pallas_call(
        functools.partial(feed_kernel, steps),
        grid=(steps + model // FEED_COLUMNS,),
        in_specs=[
            pl.BlockSpec((tokens, model), lambda i: (0, 0)),
            weight,
            weight,
            pl.BlockSpec((units, FEED_COLUMNS), lambda i: (0, jnp.maximum(i - steps, 0))),
        ],
        out_specs=pl.BlockSpec((tokens, FEED_COLUMNS), lambda i: (0, jnp.maximum(i - steps, 0))),
        out_shape=jax.ShapeDtypeStruct((tokens, model), jnp.bfloat16),
        scratch_shapes=[
            pltpu.VMEM((model, tokens), jnp.bfloat16),
            pltpu.VMEM((units, tokens), jnp.bfloat16),
        ],
        compiler_params=pltpu.CompilerParams(
            dimension_semantics=("arbitrary",), vmem_limit_bytes=48 << 20
        ),
        name="feed",
    )(x, jnp.transpose(w_gate), jnp.transpose(w_up), w_down)


def on_device(
    hidden,
    cached_len,
    attn_gain,
    query_key_value_weight,
    b_qkv,
    key_cache,
    value_cache,
    w_out,
    ffn_gain,
    w_gate,
    w_up,
    w_down,
):
    size = lax.axis_size("head")
    index_here = lax.axis_index("head")
    own_rows = hidden[0]
    fresh, model = own_rows.shape
    tokens = fresh * size
    heads_here = QUERY_HEADS // size
    row_start = index_here * fresh
    cache_length = key_cache.shape[1]
    key_start = QUERY_HEADS * HEAD_WIDTH
    coarse = max(fresh // 16, 1)

    cosine, sine = rope_tables(cached_len[0] + jnp.arange(tokens, dtype=jnp.int32))
    own_cosine = lax.dynamic_slice_in_dim(cosine, row_start, fresh, 0)[:, None, :]
    own_sine = lax.dynamic_slice_in_dim(sine, row_start, fresh, 0)[:, None, :]

    normed = gather(rms_norm(own_rows, attn_gain), size, coarse, 0).reshape(tokens, model)
    qkv_part = (
        jnp.dot(normed, query_key_value_weight, preferred_element_type=jnp.float32)
        + b_qkv.astype(jnp.float32)
    ).astype(jnp.bfloat16)
    qkv = jnp.transpose(gather(qkv_part, size, 4, 1), (1, 0, 2)).reshape(tokens, -1)
    own = lax.dynamic_slice(
        qkv, (row_start, key_start), (fresh, 2 * KEY_VALUE_HEADS * HEAD_WIDTH)
    )
    key_data = own[:, : KEY_VALUE_HEADS * HEAD_WIDTH].astype(jnp.float32)
    key_data = key_data.reshape(fresh, KEY_VALUE_HEADS, HEAD_WIDTH)
    turned = jnp.roll(key_data, HEAD_WIDTH // 2, axis=-1)
    new_keys = (key_data * own_cosine + turned * own_sine).astype(jnp.bfloat16)
    new_keys = new_keys.reshape(fresh, KEY_VALUE_HEADS * HEAD_WIDTH)
    new_values = own[:, KEY_VALUE_HEADS * HEAD_WIDTH :]

    info = jnp.stack([cached_len[0] - index_here * cache_length, row_start]).astype(jnp.int32)
    sums = attend(info, qkv, key_cache[0], value_cache[0], new_keys, new_values, cosine, sine)
    sums = sums.reshape(size, heads_here, HEAD_WIDTH + TAIL, tokens)
    mixed = scatter(sums, size, join_sums, 3)
    total = mixed[:, HEAD_WIDTH : HEAD_WIDTH + 1] + mixed[:, HEAD_WIDTH + 1 : HEAD_WIDTH + 2]
    attn = (mixed[:, :HEAD_WIDTH] / total).astype(jnp.bfloat16)
    attn = jnp.transpose(attn, (2, 0, 1)).reshape(tokens, heads_here * HEAD_WIDTH)
    projected = jnp.dot(attn, w_out, preferred_element_type=jnp.float32).astype(jnp.bfloat16)
    blocks = (size, coarse, fresh // coarse, model)
    projected = scatter(projected.reshape(blocks), size, add_blocks, 4).reshape(fresh, model)
    middle = (own_rows.astype(jnp.float32) + projected).astype(jnp.bfloat16)
    normed_two = gather(rms_norm(middle, ffn_gain), size, coarse, 5).reshape(tokens, model)
    ffn_part = feed(normed_two, w_gate, w_up, w_down)
    ffn_sum = scatter(ffn_part.reshape(blocks), size, add_blocks, 6).reshape(fresh, model)
    result = (middle.astype(jnp.float32) + ffn_sum).astype(jnp.bfloat16)
    return (result[None], new_keys[None], new_values[None])


def solution(mesh):
    in_specs = (
        P("req", "head", None),
        P("req"),
        P(),
        P(None, "head"),
        P("head"),
        P("req", "head", None),
        P("req", "head", None),
        P("head", None),
        P(),
        P(None, "head"),
        P(None, "head"),
        P("head", None),
    )
    out_specs = (P("req", "head", None), P("req", "head", None), P("req", "head", None))
    return jax.shard_map(
        on_device, mesh=mesh, in_specs=in_specs, out_specs=out_specs, check_vma=False
    )
```
